32 devices in a mesh: ctx: 4 (over y, x), head: 8 (over z, core).
Axes of the slice: x: 2, y: 2, z: 4, core: 2. Of those that a mesh axis runs over, the one named last changes fastest.
Arguments:
- queries: bfloat16 [4096, 8192], P('ctx', 'head'), may hold values from -12 to 12
- key_heads: bfloat16 [1024, 4096], P(None, 'ctx'), may hold values from -6 to 6
- value_heads: bfloat16 [1024, 4096], P(None, 'ctx'), may hold values from -6 to 6
- out_weight: bfloat16 [8192, 8192], P('head'), may hold values from -0.09375 to 0.09375
- block_order: int32 [8], replicated, may hold values from 0 to 7, each once
- doc_ids: int32 [4096], replicated, may hold values from 0 to 5, never falling along the last dimension, each value on 1 to 1024 neighbouring positions
Outputs:
- projected: bfloat16 [4096, 8192], P('ctx', 'head')
The draws below stay inside these ranges and needn't reach their ends.
Inputs may be any that keep to these rules, and one draw needn't show every extreme that they name: Layout slot j (rows j * 512 to (j + 1) * 512 - 1 of queries and projected, the same columns of key_heads and value_heads) holds block block_order[j] of the sequence; each of 0 to 7 appears once. `doc_ids`: ids never fall along the sequence; every id is used; each document holds 1 to 1024 tokens and one holds exactly 1024.
All inputs are finite; a program needn't handle non-finite values.
Results may differ from the reference program's by a relative error of at most 0.014.
Values may be sent and summed in bfloat16 or wider, within the bound.
No kernel may reach another device: no remote copies, remote signals or barrier semaphores. Data moves between devices by JAX's collectives and lax.ppermute only.
A program may use at most 192 MiB of HBM per device.

```python
import math
import jax
import jax.numpy as jnp
import numpy as np
from jax import lax

D = 8192
H = 64
KVH = 8
HD = 128
DOCS = 6
TOKENS = 4096
BLOCK = 512
BLOCKS = 8
HPD = 8
DOC_MOST = 1024


def drawn_pair(key):
    base_key = jax.random.fold_in(key, 11)
    key_query, key_keys = jax.random.split(base_key, 2)
    query_width = H * HD
    key_width = KVH * HD
    query_draw = jnp.clip(1.5 * jax.random.normal(key_query, (TOKENS, query_width), jnp.float32), -6.0, 6.0)
    key_draw = jnp.clip(1.5 * jax.random.normal(key_keys, (key_width, TOKENS), jnp.float32), -6.0, 6.0)
    return (query_draw, key_draw)


def draw_queries(key, part):
    return drawn_pair(key)[0].astype(jnp.bfloat16)


def draw_key_heads(key, part):
    return drawn_pair(key)[1].astype(jnp.bfloat16)


def with_spikes(drawn, rng, source, target, blocks, factor):
    def block_of(axis_at):
        return (jnp.arange(drawn.shape[axis_at]) // (drawn.shape[axis_at] // blocks)).reshape((-1,) + (1,) * (drawn.ndim - 1 - axis_at))

    near = jax.random.permutation(rng, blocks)[block_of(target)]
    second = (block_of(target) + blocks // 2) % blocks
    return jnp.where((block_of(source) == near) | (block_of(source) == second), factor * drawn, drawn)


def shard_levels(key, shape, shards, least, high):
    def one(axis_at, shards_of):
        draws = jax.random.uniform(jax.random.fold_in(jax.random.fold_in(key, 6), axis_at), (shards_of,), jnp.float32, least / len(shards), high / len(shards))
        return jnp.repeat(jnp.exp(draws), shape[axis_at] // shards_of).reshape((-1,) + (1,) * (len(shape) - axis_at - 1))

    level = one(*shards[0])
    for cut in shards[1:]:
        level = level * one(*cut)
    return level


def profile(number_of, total, most, lean):
    portions = [(1 << 20) // math.isqrt(rank ** lean) + 1 for rank in range(2, number_of + 1)]
    surplus, holding = total - most - (number_of - 1), [1] * (number_of - 1)
    while surplus > 0:
        movable = [i for i in range(number_of - 1) if holding[i] < most]
        mass, remaining = sum([portions[i] for i in movable]), surplus
        for i in movable:
            addition = min(most - holding[i], max(1, remaining * portions[i] // mass), surplus)
            holding[i] = holding[i] + addition
            surplus = surplus - addition
    return np.array([most] + holding)


def ragged_sizes(stream_key, amount, total, bound, lean):
    if amount == 2:
        one = jax.random.randint(stream_key, (), max(1, total - bound), min(bound, total - 1) + 1)
        return jnp.stack([one, total - one])
    tallies = jnp.asarray(profile(amount, total, bound, lean), jnp.int32)
    pairs = (amount - 1) // 2
    source_of, sink = tallies[1:1 + 2 * pairs:2], tallies[2:2 + 2 * pairs:2]
    room = jnp.minimum(source_of - 1, bound - sink)
    moved = jax.random.randint(jax.random.fold_in(stream_key, 1), (pairs,), 0, 1 << 20) % (room + 1)
    tallies = tallies.at[1:1 + 2 * pairs:2].set(source_of - moved).at[2:2 + 2 * pairs:2].set(sink + moved)
    return tallies[jax.random.permutation(jax.random.fold_in(stream_key, 2), amount)]


def bell_draw(rng, shape, width, bound, cuts=(), held_as=jnp.bfloat16):
    values = width * jax.random.normal(rng, shape, jnp.float32)
    if cuts:
        values = values * shard_levels(rng, shape, cuts, -0.22, 0.18)
    return jnp.clip(values, -bound, bound).astype(held_as)


def bell_draw_with(rng, extent, deviation, reach, cuts, heavy, held_as=jnp.bfloat16):
    result = deviation * jax.random.normal(rng, extent, jnp.float32)
    if cuts:
        result = result * shard_levels(rng, extent, cuts, -0.22, 0.18)
    return jnp.clip(with_spikes(result, jax.random.fold_in(rng, 3), *heavy), -reach, reach).astype(held_as)


def setup_inputs(seed: int = 0) -> dict:
    streams_of = jax.random.split(jax.random.key(seed), 7)
    return {
        "queries": draw_queries(jax.random.fold_in(streams_of[6], 71), 0),
        "key_heads": draw_key_heads(jax.random.fold_in(streams_of[6], 71), 0),
        "value_heads": bell_draw(streams_of[2], (KVH * HD, TOKENS), 1.0, 6.0, ((1, 4),)),
        "out_weight": bell_draw_with(streams_of[3], (H * HD, D), (H * HD) ** -0.5, 0.09375, ((0, 8),), (0, 1, 8, 2.0)),
        "block_order": jax.random.permutation(streams_of[4], BLOCKS).astype(jnp.int32),
        "doc_ids": jnp.searchsorted(jnp.cumsum(ragged_sizes(streams_of[5], DOCS, TOKENS, DOC_MOST, 0)), jnp.arange(TOKENS), side="right").astype(jnp.int32),
    }


def reference(queries, key_heads, value_heads, out_weight, block_order, doc_ids):
    row_ids = jnp.arange(TOKENS, dtype=jnp.int32)
    places = block_order[row_ids // BLOCK] * BLOCK + row_ids % BLOCK
    doc_of = doc_ids[places]
    visible = (places[None, :] <= places[:, None]) & (doc_of[None, :] == doc_of[:, None])
    share = H // KVH
    inv_root = 1.0 / math.sqrt(HD)

    def one_head(head_index):
        kv_index = head_index // share
        query_block = lax.dynamic_slice_in_dim(queries, (head_index * HD).astype(jnp.int32), HD, 1).astype(jnp.float32)
        key_block = lax.dynamic_slice_in_dim(key_heads, (kv_index * HD).astype(jnp.int32), HD, 0).astype(jnp.float32)
        value_block = lax.dynamic_slice_in_dim(value_heads, (kv_index * HD).astype(jnp.int32), HD, 0).astype(jnp.float32)
        scores = jnp.dot(query_block, key_block, precision=lax.Precision.HIGHEST) * inv_root
        scores = jnp.where(visible, scores, jnp.float32(-1e+30))
        row_top = lax.optimization_barrier(jnp.max(scores, axis=1, keepdims=True))
        unnorm = jnp.where(visible, jnp.exp(scores - row_top), jnp.float32(0.0))
        row_total = lax.optimization_barrier(jnp.sum(unnorm, axis=1, keepdims=True))
        weights = lax.optimization_barrier(unnorm.astype(jnp.bfloat16))
        mixed = jnp.dot(weights.astype(jnp.float32), value_block.T, precision=lax.Precision.HIGHEST)
        return (mixed / row_total).astype(jnp.bfloat16)
    per_head = lax.map(one_head, jnp.arange(H, dtype=jnp.int32))
    context = jnp.transpose(per_head, (1, 0, 2)).reshape(TOKENS, H * HD)
    group_width = HPD * HD

    def add_group(group_index, acc_sum):
        offset = (group_index * group_width).astype(jnp.int32)
        context_cols = lax.dynamic_slice_in_dim(context, offset, group_width, 1).astype(jnp.float32)
        weight_rows = lax.dynamic_slice_in_dim(out_weight, offset, group_width, 0).astype(jnp.float32)
        part_sum = jnp.dot(context_cols, weight_rows, precision=lax.Precision.HIGHEST).astype(jnp.bfloat16)
        part_sum = lax.optimization_barrier(part_sum)
        return acc_sum + part_sum.astype(jnp.float32)
    total_sum = lax.fori_loop(0, H // HPD, add_group, jnp.zeros((TOKENS, D), jnp.float32))
    return total_sum.astype(jnp.bfloat16)
```

```python
import functools
import math

import jax
import jax.numpy as jnp
from jax import lax
from jax.experimental import pallas as pl
from jax.experimental.pallas import tpu as pltpu
from jax.sharding import PartitionSpec as P

KVH = 8
HD = 128
DOCS = 6
FLOOR = -1e30
TQ = 256
TK = 256
MIB = 1 << 20
SMALL = pl.CostEstimate(flops=1, transcendentals=0, bytes_accessed=1)


def attend_kernel(
    row_tile, block_len, held, heads, n_pieces, scal, q_ref, *rest
):
    pieces, (o_ref, kv, acc, top, sem) = rest[:n_pieces], rest[n_pieces:]
    tile = pl.program_id(0)
    n_own = kv.shape[0]
    n_tiles_all, n_blocks = held
    inv_at = n_tiles_all
    first_at = inv_at + n_blocks
    owner_at = first_at + DOCS

    @pl.when(tile == 0)
    def _():
        copies = []
        for part in range(2):
            of_part = pieces[part * (n_pieces // 2) : (part + 1) * (n_pieces // 2)]
            sources = [piece.at[m] for piece in of_part for m in range(piece.shape[0])]
            for at, source in enumerate(sources):
                target = kv.at[scal[owner_at + at], pl.ds(part * HD, HD), :]
                copies.append(pltpu.make_async_copy(source, target, sem.at[part, at]))
        for copy in copies:
            copy.start()
        kv[:, 2 * HD :, :] = jnp.ones((n_own, HD, kv.shape[2]), kv.dtype)
        for copy in copies:
            copy.wait()

    place = scal[row_tile + tile]
    low = jnp.int32(0)
    rows = place + lax.broadcasted_iota(jnp.int32, (TQ, TK), 0)
    begin = jnp.zeros((TQ, TK), jnp.int32)
    for d in range(DOCS):
        start = scal[first_at + d]
        low = jnp.where(start <= place, start, low)
        begin = jnp.where(rows >= start, start, begin)
    acc[...] = jnp.zeros_like(acc)
    top[...] = jnp.full_like(top, FLOOR)
    scale = math.log2(math.e) / math.sqrt(HD)
    slots = kv.shape[2] // block_len

    def one(step, carry):
        base = step * TK
        slot = scal[inv_at + base // block_len]
        owner = slot // slots
        offset = pl.multiple_of((slot % slots) * block_len + base % block_len, TK)
        keys = kv[owner, 0:HD, pl.ds(offset, TK)]
        values = kv[owner, HD : 3 * HD, pl.ds(offset, TK)]
        cols = base + lax.broadcasted_iota(jnp.int32, (TQ, TK), 1)
        bias = jnp.where((cols <= rows) & (cols >= begin), 0.0, FLOOR)
        for h in range(heads):
            scores = jnp.dot(
                q_ref[:, h * HD : (h + 1) * HD], keys, preferred_element_type=jnp.float32
            )
            scores = scores * scale + bias
            old = top[h]
            new = jnp.maximum(old, jnp.max(scores, axis=1, keepdims=True))
            factor = jnp.exp2(old - new)
            weights = jnp.exp2(scores - jnp.tile(new, (1, TK // HD))).astype(jnp.bfloat16)
            mixed = lax.dot_general(
                weights, values, (((1,), (1,)), ((), ())), preferred_element_type=jnp.float32
            )
            acc[h] = acc[h] * jnp.tile(factor, (1, 2)) + mixed
            top[h] = new
        return carry

    lax.fori_loop(low // TK, (place + TQ - 1) // TK + 1, one, 0)
    for h in range(heads):
        o_ref[:, h * HD : (h + 1) * HD] = (acc[h, :, 0:HD] / acc[h, :, HD:]).astype(o_ref.dtype)


def attend(scal, queries, pieces, row_tile, n_rows, n_blocks, block_len, n_own):
    width = queries.shape[1]
    heads = width // HD
    tiles_all = queries.shape[0] // TQ
    tokens = pieces[0].shape[-1]
    return pl.pallas_call(
        functools.partial(
            attend_kernel, row_tile, block_len, (tiles_all, n_blocks), heads, len(pieces)
        ),
        out_shape=jax.ShapeDtypeStruct((n_rows, width), jnp.bfloat16),
        grid_spec=pltpu.PrefetchScalarGridSpec(
            num_scalar_prefetch=1,
            grid=(n_rows // TQ,),
            in_specs=[pl.BlockSpec((TQ, width), lambda i, s: (row_tile + i, 0))]
            + [pl.BlockSpec(memory_space=pltpu.HBM)] * len(pieces),
            out_specs=pl.BlockSpec((TQ, width), lambda i, s: (i, 0)),
            scratch_shapes=[
                pltpu.VMEM((n_own, 3 * HD, tokens), jnp.bfloat16),
                pltpu.VMEM((heads, TQ, 2 * HD), jnp.float32),
                pltpu.VMEM((heads, TQ, HD), jnp.float32),
                pltpu.SemaphoreType.DMA((2, n_own)),
            ],
        ),
        compiler_params=pltpu.CompilerParams(vmem_limit_bytes=40 * MIB),
        cost_estimate=SMALL,
        name="attend",
    )(scal, queries, *pieces)


def gather_kernel(base_ref, *rest):
    total = base_ref[...]
    for add in rest[:2]:
        total += add[...].astype(jnp.float32)
    rest[-1][...] = total.astype(rest[-1].dtype)


def gather_up(base, adds, into, total_rows, at):
    rows, width = base.shape
    tile = rows // 2
    specs = [pl.BlockSpec((tile, width), lambda i: (i, 0))] * 3
    operands = [base, *adds]
    aliases = {}
    if into is not None:
        specs.append(pl.BlockSpec(memory_space=pl.ANY))
        operands.append(into)
        aliases = {3: 0}
    return pl.pallas_call(
        gather_kernel,
        out_shape=jax.ShapeDtypeStruct((total_rows, width), jnp.bfloat16),
        grid=(2,),
        in_specs=specs,
        out_specs=pl.BlockSpec((tile, width), lambda i: (2 * at + i, 0)),
        input_output_aliases=aliases,
        cost_estimate=SMALL,
        name="gather_up",
    )(*operands)


def unit_kernel(n_add, n_out, scal, own_ref, other_ref, w_ref, wp_ref, *rest):
    adds, outs = rest[:n_add], rest[n_add:]

    def product(out):
        total = jnp.dot(own_ref[...], w_ref[...], preferred_element_type=jnp.float32)
        total += jnp.dot(other_ref[...], wp_ref[...], preferred_element_type=jnp.float32)
        for add in adds:
            total += add[...].astype(jnp.float32)
        out[...] = total.astype(out.dtype)

    for n, out in enumerate(outs):

        @pl.when((scal[1] == 1) & ((n_out == 1) | (pl.program_id(0) == n)))
        def _():
            product(out)


def in_hbm(value):
    return pltpu.with_memory_space_constraint(value, pltpu.HBM)


def unit(scal, own, other, weight, weight_p, adds, columns, tn, n_out, out_type):
    rows, depth = own.shape
    per = columns // tn

    def column(j, s):
        return j + s[2] * (1 - 2 * j) if n_out > 1 else j

    specs = [
        pl.BlockSpec((rows, depth), lambda j, s: (0, 0)),
        pl.BlockSpec((rows, depth), lambda j, s: (0, 0)),
        pl.BlockSpec((depth, tn), lambda j, s: (0, (s[0] + column(j, s)) * s[1])),
        pl.BlockSpec((depth, tn), lambda j, s: (0, (s[0] + column(j, s)) * s[1])),
    ] + [pl.BlockSpec((rows, tn), lambda j, s: (0, column(j, s) * s[1]))] * len(adds)
    out_spec = pl.BlockSpec((rows, tn), lambda j, s: (0, j if n_out == 1 else 0))
    out_shape = jax.ShapeDtypeStruct((rows, columns if n_out == 1 else tn), out_type)
    return pl.pallas_call(
        functools.partial(unit_kernel, len(adds), n_out),
        out_shape=[out_shape] * n_out,
        grid_spec=pltpu.PrefetchScalarGridSpec(
            num_scalar_prefetch=1,
            grid=(per,),
            in_specs=specs,
            out_specs=[out_spec] * n_out,
        ),
        compiler_params=pltpu.CompilerParams(vmem_limit_bytes=40 * MIB),
        cost_estimate=SMALL,
        name="unit",
    )(scal, own, other, weight, weight_p, *adds)


def own_kernel(n, scal, *refs):
    mine, other = refs[:n], refs[n : 2 * n]
    w_ref, wp_ref = refs[2 * n : 2 * n + 2]
    for a, b, out in zip(mine, other, refs[2 * n + 2 :]):
        total = jnp.dot(a[...], w_ref[...], preferred_element_type=jnp.float32)
        out[...] = total + jnp.dot(b[...], wp_ref[...], preferred_element_type=jnp.float32)


def own_product(scal, mine, other, weight, weight_p, columns):
    rows, depth = mine[0].shape
    n, tn = len(mine), 256
    per = columns // tn
    row_spec = pl.BlockSpec((rows, depth), lambda j, s: (0, 0))
    w_spec = pl.BlockSpec((depth, tn), lambda j, s: (0, s[0] * per + j))
    return pl.pallas_call(
        functools.partial(own_kernel, n),
        out_shape=[jax.ShapeDtypeStruct((rows, columns), jnp.float32)] * n,
        grid_spec=pltpu.PrefetchScalarGridSpec(
            num_scalar_prefetch=1,
            grid=(per,),
            in_specs=[row_spec] * (2 * n) + [w_spec] * 2,
            out_specs=[pl.BlockSpec((rows, tn), lambda j, s: (0, j))] * n,
        ),
        compiler_params=pltpu.CompilerParams(vmem_limit_bytes=40 * MIB),
        cost_estimate=SMALL,
        name="own_product",
    )(scal, *mine, *other, weight, weight_p)


def tables(block_order, doc_ids, row_count, owners):
    n_blocks = block_order.shape[0]
    block_len = doc_ids.shape[0] // n_blocks
    ids = jnp.arange(n_blocks, dtype=jnp.int32)
    inverse = jnp.sum(jnp.where(block_order[None, :] == ids[:, None], ids[None, :], 0), axis=1)
    first = jnp.sum(
        (doc_ids[None, :] < jnp.arange(DOCS, dtype=jnp.int32)[:, None]).astype(jnp.int32), axis=1
    )
    row = lax.axis_index("ctx") * row_count + TQ * jnp.arange(row_count // TQ, dtype=jnp.int32)
    slot = row // block_len
    start = jnp.sum(jnp.where(slot[:, None] == ids[None, :], block_order[None, :], 0), axis=1)
    places = start * block_len + row % block_len
    return jnp.concatenate([places, inverse, first, owners]).astype(jnp.int32)


def own_head(of_heads):
    group = lax.axis_size("head") // KVH
    return lax.dynamic_slice_in_dim(of_heads, lax.axis_index("head") // group * HD, HD, 0)


def general(queries, key_heads, value_heads, out_weight, block_order, doc_ids):
    row_count = queries.shape[0]
    n_own = lax.axis_size("ctx")
    n_blocks = block_order.shape[0]
    block_len = doc_ids.shape[0] // n_blocks
    gathered = [lax.all_gather(own_head(a), "ctx", axis=0) for a in (key_heads, value_heads)]
    scal = tables(block_order, doc_ids, row_count, jnp.arange(n_own, dtype=jnp.int32))
    context = attend(scal, queries, gathered, 0, row_count, n_blocks, block_len, n_own)
    partial_sum = jnp.dot(context, out_weight, preferred_element_type=jnp.float32)
    return lax.psum_scatter(
        partial_sum.astype(jnp.bfloat16), "head", scatter_dimension=1, tiled=True
    )


CHUNK = 256


def tied(value, *others):
    if not others:
        return value
    return lax.optimization_barrier((value, *others))[0]


def named(step, name):
    def run(*args):
        with jax.named_scope(name + "".join(str(a) for a in args if isinstance(a, int))):
            return step(*args)

    return run


def line(queries, key_heads, value_heads, out_weight, block_order, doc_ids):
    row_count, depth = queries.shape
    n_blocks = block_order.shape[0]
    block_len = doc_ids.shape[0] // n_blocks
    ctx, head = lax.axis_index("ctx"), lax.axis_index("head")
    chip, core = head // 2, head % 2
    far = jnp.where(core == 0, chip, 3 - chip)
    swap = [(h, h ^ 1) for h in range(8)]
    along = [[(c, c ^ k) for c in range(4)] for k in (1, 2)]

    keys, values = own_head(key_heads), own_head(value_heads)
    keys_1 = lax.ppermute(keys, "ctx", along[0])
    values_2 = lax.ppermute(values, "ctx", along[1])
    values_1 = lax.ppermute(values, "ctx", along[0])
    keys_2 = lax.ppermute(keys, "ctx", along[1])
    keys_3 = lax.ppermute(keys_1, "ctx", along[1])
    values_3 = lax.ppermute(values_2, "ctx", along[0])
    weight_p = lax.ppermute(out_weight, "head", swap)
    owners = jnp.stack([ctx, ctx ^ 1, ctx ^ 2, ctx ^ 3]).astype(jnp.int32)
    scal = tables(block_order, doc_ids, row_count, owners)
    pieces = [keys, keys_1, keys_2, keys_3, values, values_1, values_2, values_3]
    pieces = [in_hbm(p[None]) for p in pieces]
    queries = in_hbm(queries)

    chunks = row_count // CHUNK
    mine, other, base, received = {}, {}, {}, {}
    def attention(k, *behind):
        mine[k] = attend(
            tied(scal, *behind), queries, pieces, k * CHUNK // TQ, CHUNK, n_blocks, block_len, 4
        )
        other[k] = lax.ppermute(mine[k], "head", swap)

    def tick(k, s, *behind):
        valid = (far <= s) & (far <= 2)
        mirrored = 3 - s + far
        dest = jnp.where(core == 0, mirrored, 3 - mirrored)
        job = jnp.stack([jnp.where(valid, 2 * dest, 0), valid, core]).astype(jnp.int32)
        job = tied(job, *behind)
        adds = [] if s == 0 else [received[k, s - 1][0]]
        last = s == 2
        sent[k, s] = unit(
            job, mine[k], other[k], out_weight, weight_p, adds, 2 * depth, depth,
            2 if last else 1, jnp.bfloat16,
        )
        received[k, s] = []
        for cross in range(2 if last else 1):
            pairs = []
            for f in range(min(s, 2) + 1):
                pairs.append((2 * f, 2 * (f + 1) + cross))
                pairs.append((2 * (3 - f) + 1, 2 * (2 - f) + 1 - cross))
            received[k, s].append(in_hbm(lax.ppermute(sent[k, s][cross], "head", pairs)))

    own_job = jnp.stack([head, 1, 0]).astype(jnp.int32)

    def own_part(*behind):
        parts = own_product(
            tied(own_job, *behind), [in_hbm(mine[k]) for k in range(chunks)],
            [in_hbm(other[k]) for k in range(chunks)], out_weight, weight_p, depth,
        )
        base.update(enumerate(parts))

    def finish(k):
        result[0] = gather_up(base[k], received[k, 2], result[0], row_count, k)

    sent = {}
    result = [None]
    attention, tick, own_part, finish = [
        named(f, n) for f, n in ((attention, "a"), (tick, "t"), (own_part, "o"), (finish, "f"))
    ]
    attention(0)
    attention(1, mine[0])
    tick(0, 0)
    attention(2, mine[1], sent[0, 0][0])
    tick(1, 0)
    attention(3, mine[2], received[0, 0][0])
    tick(2, 0, received[0, 0][0])
    tick(3, 0, received[1, 0][0])
    for s in (1, 2):
        if s == 2:
            own_part()
        for k in range(chunks):
            tick(k, s, *([base[0]] if (k, s) == (0, 2) else []))
    for k in range(chunks):
        finish(k)
    return result[0]


def shards(*args):
    square = lax.axis_size("ctx") == 4 and lax.axis_size("head") == 8
    return (line if square else general)(*args)


def solution(mesh):
    placed = (P("ctx", "head"), P(None, "ctx"), P(None, "ctx"), P("head", None), P(), P())
    return jax.shard_map(
        shards, mesh=mesh, in_specs=placed, out_specs=P("ctx", "head"), check_vma=False
    )
```

```python
import functools
import math

import jax
import jax.numpy as jnp
from jax import lax
from jax.experimental import pallas as pl
from jax.experimental.pallas import tpu as pltpu
from jax.sharding import PartitionSpec as P

KVH = 8
HD = 128
DOCS = 6
FLOOR = -1e30
TQ = 256
TK = 256
MIB = 1 << 20
SMALL = pl.CostEstimate(flops=1, transcendentals=0, bytes_accessed=1)


def attend_kernel(
    row_tile, block_len, held, heads, n_pieces, scal, q_ref, *rest
):
    pieces, outs = rest[:n_pieces], rest[n_pieces:-4]
    kv, acc, top, sem = rest[-4:]
    tile = pl.program_id(0)
    n_own = kv.shape[0]
    n_tiles_all, n_blocks = held
    inv_at = n_tiles_all
    first_at = inv_at + n_blocks
    owner_at = first_at + DOCS

    @pl.when(tile == 0)
    def _():
        copies = []
        for part in range(2):
            of_part = pieces[part * (n_pieces // 2) : (part + 1) * (n_pieces // 2)]
            sources = [piece.at[m] for piece in of_part for m in range(piece.shape[0])]
            for at, source in enumerate(sources):
                target = kv.at[scal[owner_at + at], pl.ds(part * HD, HD), :]
                copies.append(pltpu.make_async_copy(source, target, sem.at[part, at]))
        for copy in copies:
            copy.start()
        kv[:, 2 * HD :, :] = jnp.ones((n_own, HD, kv.shape[2]), kv.dtype)
        for copy in copies:
            copy.wait()

    place = scal[row_tile + tile]
    low = jnp.int32(0)
    rows = place + lax.broadcasted_iota(jnp.int32, (TQ, TK), 0)
    begin = jnp.zeros((TQ, TK), jnp.int32)
    for d in range(DOCS):
        start = scal[first_at + d]
        low = jnp.where(start <= place, start, low)
        begin = jnp.where(rows >= start, start, begin)
    acc[...] = jnp.zeros_like(acc)
    top[...] = jnp.full_like(top, FLOOR)
    scale = math.log2(math.e) / math.sqrt(HD)
    slots = kv.shape[2] // block_len

    def one(step, carry):
        base = step * TK
        slot = scal[inv_at + base // block_len]
        owner = slot // slots
        offset = pl.multiple_of((slot % slots) * block_len + base % block_len, TK)
        keys = kv[owner, 0:HD, pl.ds(offset, TK)]
        values = kv[owner, HD : 3 * HD, pl.ds(offset, TK)]
        cols = base + lax.broadcasted_iota(jnp.int32, (TQ, TK), 1)
        bias = jnp.where((cols <= rows) & (cols >= begin), 0.0, FLOOR)
        for h in range(heads):
            scores = jnp.dot(
                q_ref[:, h * HD : (h + 1) * HD], keys, preferred_element_type=jnp.float32
            )
            scores = scores * scale + bias
            old = top[h]
            new = jnp.maximum(old, jnp.max(scores, axis=1, keepdims=True))
            factor = jnp.exp2(old - new)
            weights = jnp.exp2(scores - jnp.tile(new, (1, TK // HD))).astype(jnp.bfloat16)
            mixed = lax.dot_general(
                weights, values, (((1,), (1,)), ((), ())), preferred_element_type=jnp.float32
            )
            acc[h] = acc[h] * jnp.tile(factor, (1, 2)) + mixed
            top[h] = new
        return carry

    lax.fori_loop(low // TK, (place + TQ - 1) // TK + 1, one, 0)
    for n, out in enumerate(outs):

        @pl.when((len(outs) == 1) | (tile == n))
        def _():
            for h in range(heads):
                out[:, h * HD : (h + 1) * HD] = (acc[h, :, 0:HD] / acc[h, :, HD:]).astype(out.dtype)


def attend(scal, queries, pieces, row_tile, n_rows, n_blocks, block_len, n_own, n_out=1):
    width = queries.shape[1]
    heads = width // HD
    tiles_all = queries.shape[0] // TQ
    tokens = pieces[0].shape[-1]
    return pl.pallas_call(
        functools.partial(
            attend_kernel, row_tile, block_len, (tiles_all, n_blocks), heads, len(pieces)
        ),
        out_shape=[jax.ShapeDtypeStruct((n_rows // n_out, width), jnp.bfloat16)] * n_out,
        grid_spec=pltpu.PrefetchScalarGridSpec(
            num_scalar_prefetch=1,
            grid=(n_rows // TQ,),
            in_specs=[pl.BlockSpec((TQ, width), lambda i, s: (row_tile + i, 0))]
            + [pl.BlockSpec(memory_space=pltpu.HBM)] * len(pieces),
            out_specs=[pl.BlockSpec((TQ, width), lambda i, s: (i if n_out == 1 else 0, 0))] * n_out,
            scratch_shapes=[
                pltpu.VMEM((n_own, 3 * HD, tokens), jnp.bfloat16),
                pltpu.VMEM((heads, TQ, 2 * HD), jnp.float32),
                pltpu.VMEM((heads, TQ, HD), jnp.float32),
                pltpu.SemaphoreType.DMA((2, n_own)),
            ],
        ),
        compiler_params=pltpu.CompilerParams(vmem_limit_bytes=40 * MIB),
        cost_estimate=SMALL,
        name="attend",
    )(scal, queries, *pieces)


def gather_kernel(base_ref, *rest):
    total = base_ref[...]
    for add in rest[:2]:
        total += add[...].astype(jnp.float32)
    rest[-1][...] = total.astype(rest[-1].dtype)


def gather_up(base, adds, into, total_rows, at):
    rows, width = base.shape
    tile = rows // 2
    specs = [pl.BlockSpec((tile, width), lambda i: (i, 0))] * 3
    operands = [base, *adds]
    aliases = {}
    if into is not None:
        specs.append(pl.BlockSpec(memory_space=pl.ANY))
        operands.append(into)
        aliases = {3: 0}
    return pl.pallas_call(
        gather_kernel,
        out_shape=jax.ShapeDtypeStruct((total_rows, width), jnp.bfloat16),
        grid=(2,),
        in_specs=specs,
        out_specs=pl.BlockSpec((tile, width), lambda i: (2 * at + i, 0)),
        input_output_aliases=aliases,
        cost_estimate=SMALL,
        name="gather_up",
    )(*operands)


def unit_kernel(n_add, n_out, scal, own_ref, other_ref, w_ref, wp_ref, *rest):
    adds, outs = rest[:n_add], rest[n_add:]

    def product(out):
        total = jnp.dot(own_ref[...], w_ref[...], preferred_element_type=jnp.float32)
        total += jnp.dot(other_ref[...], wp_ref[...], preferred_element_type=jnp.float32)
        for add in adds:
            total += add[...].astype(jnp.float32)
        out[...] = total.astype(out.dtype)

    for n, out in enumerate(outs):

        @pl.when((scal[1] == 1) & ((n_out == 1) | (pl.program_id(0) == n)))
        def _():
            product(out)


def in_hbm(value):
    return pltpu.with_memory_space_constraint(value, pltpu.HBM)


def unit(scal, own, other, weight, weight_p, adds, columns, tn, n_out, out_type):
    rows, depth = own.shape
    per = columns // tn

    def column(j, s):
        return j + s[2] * (1 - 2 * j) if n_out > 1 else j

    specs = [
        pl.BlockSpec((rows, depth), lambda j, s: (0, 0)),
        pl.BlockSpec((rows, depth), lambda j, s: (0, 0)),
        pl.BlockSpec((depth, tn), lambda j, s: (0, (s[0] + column(j, s)) * s[1])),
        pl.BlockSpec((depth, tn), lambda j, s: (0, (s[0] + column(j, s)) * s[1])),
    ] + [pl.BlockSpec((rows, tn), lambda j, s: (0, column(j, s) * s[1]))] * len(adds)
    out_spec = pl.BlockSpec((rows, tn), lambda j, s: (0, j if n_out == 1 else 0))
    out_shape = jax.ShapeDtypeStruct((rows, columns if n_out == 1 else tn), out_type)
    return pl.pallas_call(
        functools.partial(unit_kernel, len(adds), n_out),
        out_shape=[out_shape] * n_out,
        grid_spec=pltpu.PrefetchScalarGridSpec(
            num_scalar_prefetch=1,
            grid=(per,),
            in_specs=specs,
            out_specs=[out_spec] * n_out,
        ),
        compiler_params=pltpu.CompilerParams(vmem_limit_bytes=40 * MIB),
        cost_estimate=SMALL,
        name="unit",
    )(scal, own, other, weight, weight_p, *adds)


def own_kernel(n, scal, *refs):
    mine, other = refs[:n], refs[n : 2 * n]
    w_ref, wp_ref = refs[2 * n : 2 * n + 2]
    for a, b, out in zip(mine, other, refs[2 * n + 2 :]):
        total = jnp.dot(a[...], w_ref[...], preferred_element_type=jnp.float32)
        out[...] = total + jnp.dot(b[...], wp_ref[...], preferred_element_type=jnp.float32)


def own_product(scal, mine, other, weight, weight_p, columns):
    rows, depth = mine[0].shape
    n, tn = len(mine), 256
    per = columns // tn
    row_spec = pl.BlockSpec((rows, depth), lambda j, s: (0, 0))
    w_spec = pl.BlockSpec((depth, tn), lambda j, s: (0, s[0] * per + j))
    return pl.pallas_call(
        functools.partial(own_kernel, n),
        out_shape=[jax.ShapeDtypeStruct((rows, columns), jnp.float32)] * n,
        grid_spec=pltpu.PrefetchScalarGridSpec(
            num_scalar_prefetch=1,
            grid=(per,),
            in_specs=[row_spec] * (2 * n) + [w_spec] * 2,
            out_specs=[pl.BlockSpec((rows, tn), lambda j, s: (0, j))] * n,
        ),
        compiler_params=pltpu.CompilerParams(vmem_limit_bytes=40 * MIB),
        cost_estimate=SMALL,
        name="own_product",
    )(scal, *mine, *other, weight, weight_p)


def tables(block_order, doc_ids, row_count, owners):
    n_blocks = block_order.shape[0]
    block_len = doc_ids.shape[0] // n_blocks
    ids = jnp.arange(n_blocks, dtype=jnp.int32)
    inverse = jnp.sum(jnp.where(block_order[None, :] == ids[:, None], ids[None, :], 0), axis=1)
    first = jnp.sum(
        (doc_ids[None, :] < jnp.arange(DOCS, dtype=jnp.int32)[:, None]).astype(jnp.int32), axis=1
    )
    row = lax.axis_index("ctx") * row_count + TQ * jnp.arange(row_count // TQ, dtype=jnp.int32)
    slot = row // block_len
    start = jnp.sum(jnp.where(slot[:, None] == ids[None, :], block_order[None, :], 0), axis=1)
    places = start * block_len + row % block_len
    return jnp.concatenate([places, inverse, first, owners]).astype(jnp.int32)


def own_head(of_heads):
    group = lax.axis_size("head") // KVH
    return lax.dynamic_slice_in_dim(of_heads, lax.axis_index("head") // group * HD, HD, 0)


def general(queries, key_heads, value_heads, out_weight, block_order, doc_ids):
    row_count = queries.shape[0]
    n_own = lax.axis_size("ctx")
    n_blocks = block_order.shape[0]
    block_len = doc_ids.shape[0] // n_blocks
    gathered = [lax.all_gather(own_head(a), "ctx", axis=0) for a in (key_heads, value_heads)]
    scal = tables(block_order, doc_ids, row_count, jnp.arange(n_own, dtype=jnp.int32))
    context = attend(scal, queries, gathered, 0, row_count, n_blocks, block_len, n_own)[0]
    partial_sum = jnp.dot(context, out_weight, preferred_element_type=jnp.float32)
    return lax.psum_scatter(
        partial_sum.astype(jnp.bfloat16), "head", scatter_dimension=1, tiled=True
    )


CHUNK = 256


def tied(value, *others):
    if not others:
        return value
    return lax.optimization_barrier((value, *others))[0]


def named(step, name):
    def run(*args, **kw):
        with jax.named_scope(name + "".join(str(a) for a in args if isinstance(a, int))):
            return step(*args, **kw)

    return run


def line(queries, key_heads, value_heads, out_weight, block_order, doc_ids):
    row_count, depth = queries.shape
    n_blocks = block_order.shape[0]
    block_len = doc_ids.shape[0] // n_blocks
    ctx, head = lax.axis_index("ctx"), lax.axis_index("head")
    chip, core = head // 2, head % 2
    far = jnp.where(core == 0, chip, 3 - chip)
    swap = [(h, h ^ 1) for h in range(8)]
    along = [[(c, c ^ k) for c in range(4)] for k in (1, 2)]

    keys, values = own_head(key_heads), own_head(value_heads)
    keys_1 = lax.ppermute(keys, "ctx", along[0])
    values_2 = lax.ppermute(values, "ctx", along[1])
    values_1 = lax.ppermute(values, "ctx", along[0])
    keys_2 = lax.ppermute(keys, "ctx", along[1])
    keys_3 = lax.ppermute(keys_1, "ctx", along[1])
    values_3 = lax.ppermute(values_2, "ctx", along[0])
    weight_p = lax.ppermute(out_weight, "head", swap)
    owners = jnp.stack([ctx, ctx ^ 1, ctx ^ 2, ctx ^ 3]).astype(jnp.int32)
    scal = tables(block_order, doc_ids, row_count, owners)
    pieces = [keys, keys_1, keys_2, keys_3, values, values_1, values_2, values_3]
    pieces = [in_hbm(p[None]) for p in pieces]
    queries = in_hbm(queries)

    chunks = row_count // CHUNK
    mine, other, base, received = {}, {}, {}, {}
    def attention(k, *behind, count=1):
        found = attend(
            tied(scal, *behind), queries, pieces, k * CHUNK // TQ, count * CHUNK, n_blocks,
            block_len, 4, count,
        )
        for n in range(count):
            mine[k + n] = found[n]
            other[k + n] = lax.ppermute(found[n], "head", swap)

    def tick(k, s, *behind):
        valid = (far <= s) & (far <= 2)
        mirrored = 3 - s + far
        dest = jnp.where(core == 0, mirrored, 3 - mirrored)
        job = jnp.stack([jnp.where(valid, 2 * dest, 0), valid, core]).astype(jnp.int32)
        job = tied(job, *behind)
        adds = [] if s == 0 else [received[k, s - 1][0]]
        last = s == 2
        sent[k, s] = unit(
            job, mine[k], other[k], out_weight, weight_p, adds, 2 * depth, depth,
            2 if last else 1, jnp.bfloat16,
        )
        received[k, s] = []
        for cross in range(2 if last else 1):
            pairs = []
            for f in range(min(s, 2) + 1):
                pairs.append((2 * f, 2 * (f + 1) + cross))
                pairs.append((2 * (3 - f) + 1, 2 * (2 - f) + 1 - cross))
            received[k, s].append(in_hbm(lax.ppermute(sent[k, s][cross], "head", pairs)))

    own_job = jnp.stack([head, 1, 0]).astype(jnp.int32)

    def own_part(*behind):
        parts = own_product(
            tied(own_job, *behind), [in_hbm(mine[k]) for k in range(chunks)],
            [in_hbm(other[k]) for k in range(chunks)], out_weight, weight_p, depth,
        )
        base.update(enumerate(parts))

    def finish(k):
        result[0] = gather_up(base[k], received[k, 2], result[0], row_count, k)

    sent = {}
    result = [None]
    attention, tick, own_part, finish = [
        named(f, n) for f, n in ((attention, "a"), (tick, "t"), (own_part, "o"), (finish, "f"))
    ]
    attention(0)
    attention(1, mine[0])
    tick(0, 0)
    tick(1, 0)
    attention(2, mine[1], sent[1, 0][0], count=2)
    tick(2, 0, received[0, 0][0])
    tick(3, 0, received[1, 0][0])
    for s in (1, 2):
        if s == 2:
            own_part()
        for k in range(chunks):
            tick(k, s, *([base[0]] if (k, s) == (0, 2) else []))
    for k in range(chunks):
        finish(k)
    return result[0]


def shards(*args):
    square = lax.axis_size("ctx") == 4 and lax.axis_size("head") == 8
    return (line if square else general)(*args)


def solution(mesh):
    placed = (P("ctx", "head"), P(None, "ctx"), P(None, "ctx"), P("head", None), P(), P())
    return jax.shard_map(
        shards, mesh=mesh, in_specs=placed, out_specs=P("ctx", "head"), check_vma=False
    )
```

```python
import functools
import math

import jax
import jax.numpy as jnp
from jax import lax
from jax.experimental import pallas as pl
from jax.experimental.pallas import tpu as pltpu
from jax.sharding import PartitionSpec as P

KVH = 8
HD = 128
DOCS = 6
FLOOR = -1e30
TQ = 256
TK = 256
MIB = 1 << 20
SMALL = pl.CostEstimate(flops=1, transcendentals=0, bytes_accessed=1)


def attend_kernel(
    row_tile, block_len, held, heads, n_pieces, scal, q_ref, *rest
):
    pieces, outs = rest[:n_pieces], rest[n_pieces:-4]
    kv, acc, top, sem = rest[-4:]
    tile = pl.program_id(0)
    n_own = kv.shape[0]
    n_tiles_all, n_blocks = held
    inv_at = n_tiles_all
    first_at = inv_at + n_blocks
    owner_at = first_at + DOCS

    @pl.when(tile == 0)
    def _():
        copies = []
        for part in range(2):
            of_part = pieces[part * (n_pieces // 2) : (part + 1) * (n_pieces // 2)]
            sources = [piece.at[m] for piece in of_part for m in range(piece.shape[0])]
            for at, source in enumerate(sources):
                target = kv.at[scal[owner_at + at], pl.ds(part * HD, HD), :]
                copies.append(pltpu.make_async_copy(source, target, sem.at[part, at]))
        for copy in copies:
            copy.start()
        kv[:, 2 * HD :, :] = jnp.ones((n_own, HD, kv.shape[2]), kv.dtype)
        for copy in copies:
            copy.wait()

    place = scal[row_tile + tile]
    low = jnp.int32(0)
    rows = place + lax.broadcasted_iota(jnp.int32, (TQ, TK), 0)
    begin = jnp.zeros((TQ, TK), jnp.int32)
    for d in range(DOCS):
        start = scal[first_at + d]
        low = jnp.where(start <= place, start, low)
        begin = jnp.where(rows >= start, start, begin)
    acc[...] = jnp.zeros_like(acc)
    top[...] = jnp.full_like(top, FLOOR)
    scale = math.log2(math.e) / math.sqrt(HD)
    slots = kv.shape[2] // block_len

    def one(step, carry):
        base = step * TK
        slot = scal[inv_at + base // block_len]
        owner = slot // slots
        offset = pl.multiple_of((slot % slots) * block_len + base % block_len, TK)
        keys = kv[owner, 0:HD, pl.ds(offset, TK)]
        values = kv[owner, HD : 3 * HD, pl.ds(offset, TK)]
        cols = base + lax.broadcasted_iota(jnp.int32, (TQ, TK), 1)
        bias = jnp.where((cols <= rows) & (cols >= begin), 0.0, FLOOR)
        for h in range(heads):
            scores = jnp.dot(
                q_ref[:, h * HD : (h + 1) * HD], keys, preferred_element_type=jnp.float32
            )
            scores = scores * scale + bias
            old = top[h]
            new = jnp.maximum(old, jnp.max(scores, axis=1, keepdims=True))
            factor = jnp.exp2(old - new)
            weights = jnp.exp2(scores - jnp.tile(new, (1, TK // HD))).astype(jnp.bfloat16)
            mixed = lax.dot_general(
                weights, values, (((1,), (1,)), ((), ())), preferred_element_type=jnp.float32
            )
            acc[h] = acc[h] * jnp.tile(factor, (1, 2)) + mixed
            top[h] = new
        return carry

    lax.fori_loop(low // TK, (place + TQ - 1) // TK + 1, one, 0)
    for n, out in enumerate(outs):

        @pl.when((len(outs) == 1) | (tile == n))
        def _():
            for h in range(heads):
                out[:, h * HD : (h + 1) * HD] = (acc[h, :, 0:HD] / acc[h, :, HD:]).astype(out.dtype)


def attend(scal, queries, pieces, row_tile, n_rows, n_blocks, block_len, n_own, n_out=1):
    width = queries.shape[1]
    heads = width // HD
    tiles_all = queries.shape[0] // TQ
    tokens = pieces[0].shape[-1]
    return pl.pallas_call(
        functools.partial(
            attend_kernel, row_tile, block_len, (tiles_all, n_blocks), heads, len(pieces)
        ),
        out_shape=[jax.ShapeDtypeStruct((n_rows // n_out, width), jnp.bfloat16)] * n_out,
        grid_spec=pltpu.PrefetchScalarGridSpec(
            num_scalar_prefetch=1,
            grid=(n_rows // TQ,),
            in_specs=[pl.BlockSpec((TQ, width), lambda i, s: (row_tile + i, 0))]
            + [pl.BlockSpec(memory_space=pltpu.HBM)] * len(pieces),
            out_specs=[pl.BlockSpec((TQ, width), lambda i, s: (i if n_out == 1 else 0, 0))] * n_out,
            scratch_shapes=[
                pltpu.VMEM((n_own, 3 * HD, tokens), jnp.bfloat16),
                pltpu.VMEM((heads, TQ, 2 * HD), jnp.float32),
                pltpu.VMEM((heads, TQ, HD), jnp.float32),
                pltpu.SemaphoreType.DMA((2, n_own)),
            ],
        ),
        compiler_params=pltpu.CompilerParams(vmem_limit_bytes=40 * MIB),
        cost_estimate=SMALL,
        name="attend",
    )(scal, queries, *pieces)


def gather_kernel(base_ref, *rest):
    total = base_ref[...]
    for add in rest[:2]:
        total += add[...].astype(jnp.float32)
    rest[-1][...] = total.astype(rest[-1].dtype)


def gather_up(base, adds, into, total_rows, at):
    rows, width = base.shape
    tile = rows // 2
    specs = [pl.BlockSpec((tile, width), lambda i: (i, 0))] * 3
    operands = [base, *adds]
    aliases = {}
    if into is not None:
        specs.append(pl.BlockSpec(memory_space=pl.ANY))
        operands.append(into)
        aliases = {3: 0}
    return pl.pallas_call(
        gather_kernel,
        out_shape=jax.ShapeDtypeStruct((total_rows, width), jnp.bfloat16),
        grid=(2,),
        in_specs=specs,
        out_specs=pl.BlockSpec((tile, width), lambda i: (2 * at + i, 0)),
        input_output_aliases=aliases,
        cost_estimate=SMALL,
        name="gather_up",
    )(*operands)


def unit_kernel(n_add, n_out, scal, own_ref, other_ref, w_ref, wp_ref, *rest):
    adds, outs = rest[:n_add], rest[n_add:]

    def product(out):
        total = jnp.dot(own_ref[...], w_ref[...], preferred_element_type=jnp.float32)
        total += jnp.dot(other_ref[...], wp_ref[...], preferred_element_type=jnp.float32)
        for add in adds:
            total += add[...].astype(jnp.float32)
        out[...] = total.astype(out.dtype)

    for n, out in enumerate(outs):

        @pl.when((scal[1] == 1) & ((n_out == 1) | (pl.program_id(0) == n)))
        def _():
            product(out)


def in_hbm(value):
    return pltpu.with_memory_space_constraint(value, pltpu.HBM)


def unit(scal, own, other, weight, weight_p, adds, columns, tn, n_out, out_type):
    rows, depth = own.shape
    per = columns // tn

    def column(j, s):
        return j + s[2] * (1 - 2 * j) if n_out > 1 else j

    specs = [
        pl.BlockSpec((rows, depth), lambda j, s: (0, 0)),
        pl.BlockSpec((rows, depth), lambda j, s: (0, 0)),
        pl.BlockSpec((depth, tn), lambda j, s: (0, (s[0] + column(j, s)) * s[1])),
        pl.BlockSpec((depth, tn), lambda j, s: (0, (s[0] + column(j, s)) * s[1])),
    ] + [pl.BlockSpec((rows, tn), lambda j, s: (0, column(j, s) * s[1]))] * len(adds)
    out_spec = pl.BlockSpec((rows, tn), lambda j, s: (0, j if n_out == 1 else 0))
    out_shape = jax.ShapeDtypeStruct((rows, columns if n_out == 1 else tn), out_type)
    return pl.pallas_call(
        functools.partial(unit_kernel, len(adds), n_out),
        out_shape=[out_shape] * n_out,
        grid_spec=pltpu.PrefetchScalarGridSpec(
            num_scalar_prefetch=1,
            grid=(per,),
            in_specs=specs,
            out_specs=[out_spec] * n_out,
        ),
        compiler_params=pltpu.CompilerParams(vmem_limit_bytes=40 * MIB),
        cost_estimate=SMALL,
        name="unit",
    )(scal, own, other, weight, weight_p, *adds)


def own_kernel(n, scal, *refs):
    mine, other = refs[:n], refs[n : 2 * n]
    w_ref, wp_ref = refs[2 * n : 2 * n + 2]
    for a, b, out in zip(mine, other, refs[2 * n + 2 :]):
        total = jnp.dot(a[...], w_ref[...], preferred_element_type=jnp.float32)
        out[...] = total + jnp.dot(b[...], wp_ref[...], preferred_element_type=jnp.float32)


def own_product(scal, mine, other, weight, weight_p, columns):
    rows, depth = mine[0].shape
    n, tn = len(mine), 256
    per = columns // tn
    row_spec = pl.BlockSpec((rows, depth), lambda j, s: (0, 0))
    w_spec = pl.BlockSpec((depth, tn), lambda j, s: (0, s[0] * per + j))
    return pl.pallas_call(
        functools.partial(own_kernel, n),
        out_shape=[jax.ShapeDtypeStruct((rows, columns), jnp.float32)] * n,
        grid_spec=pltpu.PrefetchScalarGridSpec(
            num_scalar_prefetch=1,
            grid=(per,),
            in_specs=[row_spec] * (2 * n) + [w_spec] * 2,
            out_specs=[pl.BlockSpec((rows, tn), lambda j, s: (0, j))] * n,
        ),
        compiler_params=pltpu.CompilerParams(vmem_limit_bytes=40 * MIB),
        cost_estimate=SMALL,
        name="own_product",
    )(scal, *mine, *other, weight, weight_p)


def tables(block_order, doc_ids, row_count, owners):
    n_blocks = block_order.shape[0]
    block_len = doc_ids.shape[0] // n_blocks
    ids = jnp.arange(n_blocks, dtype=jnp.int32)
    inverse = jnp.sum(jnp.where(block_order[None, :] == ids[:, None], ids[None, :], 0), axis=1)
    first = jnp.sum(
        (doc_ids[None, :] < jnp.arange(DOCS, dtype=jnp.int32)[:, None]).astype(jnp.int32), axis=1
    )
    row = lax.axis_index("ctx") * row_count + TQ * jnp.arange(row_count // TQ, dtype=jnp.int32)
    slot = row // block_len
    start = jnp.sum(jnp.where(slot[:, None] == ids[None, :], block_order[None, :], 0), axis=1)
    places = start * block_len + row % block_len
    return jnp.concatenate([places, inverse, first, owners]).astype(jnp.int32)


def own_head(of_heads):
    group = lax.axis_size("head") // KVH
    return lax.dynamic_slice_in_dim(of_heads, lax.axis_index("head") // group * HD, HD, 0)


def general(queries, key_heads, value_heads, out_weight, block_order, doc_ids):
    row_count = queries.shape[0]
    n_own = lax.axis_size("ctx")
    n_blocks = block_order.shape[0]
    block_len = doc_ids.shape[0] // n_blocks
    gathered = [lax.all_gather(own_head(a), "ctx", axis=0) for a in (key_heads, value_heads)]
    scal = tables(block_order, doc_ids, row_count, jnp.arange(n_own, dtype=jnp.int32))
    context = attend(scal, queries, gathered, 0, row_count, n_blocks, block_len, n_own)[0]
    partial_sum = jnp.dot(context, out_weight, preferred_element_type=jnp.float32)
    return lax.psum_scatter(
        partial_sum.astype(jnp.bfloat16), "head", scatter_dimension=1, tiled=True
    )


CHUNK = 256


def tied(value, *others):
    if not others:
        return value
    return lax.optimization_barrier((value, *others))[0]


def named(step, name):
    def run(*args, **kw):
        with jax.named_scope(name + "".join(str(a) for a in args if isinstance(a, int))):
            return step(*args, **kw)

    return run


def line(queries, key_heads, value_heads, out_weight, block_order, doc_ids):
    row_count, depth = queries.shape
    n_blocks = block_order.shape[0]
    block_len = doc_ids.shape[0] // n_blocks
    ctx, head = lax.axis_index("ctx"), lax.axis_index("head")
    chip, core = head // 2, head % 2
    far = jnp.where(core == 0, chip, 3 - chip)
    swap = [(h, h ^ 1) for h in range(8)]
    along = [[(c, c ^ k) for c in range(4)] for k in (1, 2)]

    keys, values = own_head(key_heads), own_head(value_heads)
    keys_1 = lax.ppermute(keys, "ctx", along[0])
    values_2 = lax.ppermute(values, "ctx", along[1])
    values_1 = lax.ppermute(values, "ctx", along[0])
    keys_2 = lax.ppermute(keys, "ctx", along[1])
    keys_3 = lax.ppermute(keys_1, "ctx", along[1])
    values_3 = lax.ppermute(values_2, "ctx", along[0])
    weight_p = lax.ppermute(out_weight, "head", swap)
    owners = jnp.stack([ctx, ctx ^ 1, ctx ^ 2, ctx ^ 3]).astype(jnp.int32)
    scal = tables(block_order, doc_ids, row_count, owners)
    pieces = [keys, keys_1, keys_2, keys_3, values, values_1, values_2, values_3]
    pieces = [in_hbm(p[None]) for p in pieces]
    queries = in_hbm(queries)

    chunks = row_count // CHUNK
    mine, other, base, received = {}, {}, {}, {}
    def attention(k, *behind, count=1):
        found = attend(
            tied(scal, *behind), queries, pieces, k * CHUNK // TQ, count * CHUNK, n_blocks,
            block_len, 4, count,
        )
        for n in range(count):
            mine[k + n] = found[n]
            other[k + n] = lax.ppermute(found[n], "head", swap)

    def tick(k, s, *behind):
        valid = (far <= s) & (far <= 2)
        mirrored = 3 - s + far
        dest = jnp.where(core == 0, mirrored, 3 - mirrored)
        job = jnp.stack([jnp.where(valid, 2 * dest, 0), valid, core]).astype(jnp.int32)
        job = tied(job, *behind)
        adds = [] if s == 0 else [received[k, s - 1][0]]
        last = s == 2
        sent[k, s] = unit(
            job, mine[k], other[k], out_weight, weight_p, adds, 2 * depth, depth,
            2 if last else 1, jnp.bfloat16,
        )
        received[k, s] = []
        for cross in range(2 if last else 1):
            pairs = []
            for f in range(min(s, 2) + 1):
                pairs.append((2 * f, 2 * (f + 1) + cross))
                pairs.append((2 * (3 - f) + 1, 2 * (2 - f) + 1 - cross))
            received[k, s].append(in_hbm(lax.ppermute(sent[k, s][cross], "head", pairs)))

    own_job = jnp.stack([head, 1, 0]).astype(jnp.int32)

    def own_part(*behind):
        parts = own_product(
            tied(own_job, *behind), [in_hbm(mine[k]) for k in range(chunks)],
            [in_hbm(other[k]) for k in range(chunks)], out_weight, weight_p, depth,
        )
        base.update(enumerate(parts))

    def finish(k):
        result[0] = gather_up(base[k], received[k, 2], result[0], row_count, k)

    sent = {}
    result = [None]
    attention, tick, own_part, finish = [
        named(f, n) for f, n in ((attention, "a"), (tick, "t"), (own_part, "o"), (finish, "f"))
    ]
    attention(0, count=2)
    tick(0, 0)
    tick(1, 0)
    attention(2, mine[1], sent[1, 0][0], count=2)
    tick(2, 0, received[0, 0][0])
    tick(3, 0, received[1, 0][0])
    for s in (1, 2):
        if s == 2:
            own_part()
        for k in range(chunks):
            tick(k, s, *([base[0]] if (k, s) == (0, 2) else []))
    for k in range(chunks):
        finish(k)
    return result[0]


def shards(*args):
    square = lax.axis_size("ctx") == 4 and lax.axis_size("head") == 8
    return (line if square else general)(*args)


def solution(mesh):
    placed = (P("ctx", "head"), P(None, "ctx"), P(None, "ctx"), P("head", None), P(), P())
    return jax.shard_map(
        shards, mesh=mesh, in_specs=placed, out_specs=P("ctx", "head"), check_vma=False
    )
```
